32 devices in a mesh: table: 16 (over z, y, x), tensor: 2 (over core).
Axes of the slice: x: 2, y: 2, z: 4, core: 2. Of those that a mesh axis runs over, the one named last changes fastest.
Arguments:
- hidden: bfloat16 [512, 2560], P('table'), may hold values from -16 to 16
- attn_gain: float32 [2560], replicated, may hold values from 0.6 to 1.4
- q_weight: bfloat16 [2560, 2560], P(None, 'tensor'), may hold values from -1 to 1
- kv_weight: bfloat16 [2560, 2, 512], P(None, None, 'tensor'), may hold values from -0.125 to 0.125
- out_weight: bfloat16 [2560, 2560], P('tensor'), may hold values from -0.125 to 0.125
- key_cache: bfloat16 [512, 256, 512], P('table', None, 'tensor'), may hold values from -256 to 256
- value_cache: bfloat16 [512, 256, 512], P('table', None, 'tensor'), may hold values from -6 to 6
- cache_lengths: int32 [512], P('table'), may hold values from 64 to 256
- table: bfloat16 [65536, 1280], P('table'), may hold values from -6 to 6
- key_proj: bfloat16 [1280, 2560], P(None, 'tensor'), may hold values from -0.15625 to 0.15625
- value_proj: bfloat16 [1280, 2560], P(None, 'tensor'), may hold values from -0.15625 to 0.15625
- lookup_ids: int32 [512, 16], P('table'), may hold values from 0 to 65535, as said below
Outputs:
- mixed: bfloat16 [512, 2560], P('table', 'tensor')
The draws below stay inside these ranges and needn't reach their ends.
Inputs may be any that keep to these rules, and one draw needn't show every extreme that they name: `lookup_ids`: within the 32 sequences of one index of table (aligned blocks of rows), at most 64 ids lie in the range of 4096 rows of any one owner (owner = id // 4096); in every draw one owner gets exactly 64 ids from every block.
All inputs are finite; a program needn't handle non-finite values.
Results may differ from the reference program's by a relative error of at most 0.007.
Values may be sent and summed in bfloat16 or wider, within the bound.
A program may use at most 128 MiB of HBM per device.

```python
import math
import jax
import jax.numpy as jnp
from jax import lax

D = 2560
EMB = 1280
HEADS = 20
KV_HEADS = 4
HEAD_DIM = 128
LOOKUPS = 16
SEQ_DEV = 32
CTX = 256
ROWS_DEV = 4096
SEQS = 512
ROWS = 65536
CAP = 64
N_TABLE = 16


def joint_draw(key):
    base_key = jax.random.fold_in(key, 5)
    subkeys = jax.random.split(base_key, 6)
    col_scale = jnp.exp(jax.random.uniform(subkeys[0], (1, D), jnp.float32, math.log(0.5), math.log(2.0)))
    hidden = jax.random.normal(subkeys[1], (SEQS, D), jnp.float32) * col_scale
    hidden = jnp.clip(hidden, -16.0, 16.0)
    gain_draw = jax.random.uniform(subkeys[3], (D,), jnp.float32, 0.6, 1.4)
    query_weight = jnp.clip(jax.random.normal(subkeys[4], (D, HEADS * HEAD_DIM), jnp.float32) / math.sqrt(D), -1.0, 1.0)
    key_draw = jax.random.normal(subkeys[5], (SEQS, CTX, KV_HEADS * HEAD_DIM), jnp.float32)
    key_draw = jnp.clip(key_draw, -256.0, 256.0)
    return (hidden, gain_draw, query_weight, key_draw)


def draw_hidden(key, part):
    return joint_draw(key)[0].astype(jnp.bfloat16)


def draw_attn_gain(key, part):
    return joint_draw(key)[1].astype(jnp.float32)


def draw_q_weight(key, part):
    return joint_draw(key)[2].astype(jnp.bfloat16)


def draw_key_cache(key, part):
    return joint_draw(key)[3].astype(jnp.bfloat16)


def draw_lookup_ids(key, part):
    base_key = jax.random.fold_in(key, 11)
    subkeys = jax.random.split(base_key, 4)
    requests = SEQ_DEV * LOOKUPS
    position_total = N_TABLE * CAP
    heaviest_holder = jax.random.randint(subkeys[0], (), 0, N_TABLE)
    position_number = jnp.arange(position_total, dtype=jnp.int32)
    holder_by_position = position_number // CAP
    energy_offset = jnp.where(holder_by_position == heaviest_holder, 1 << 17, 0).astype(jnp.int32)
    attention_energies = jax.random.randint(subkeys[1], (N_TABLE, position_total), 0, 1 << 16)
    combined_result = (attention_energies + energy_offset[None, :]) * position_total + position_number[None, :]
    picked = lax.top_k(combined_result, requests)[1]
    owner_of = (picked // CAP).astype(jnp.int32)
    shuffle_keys = jax.random.randint(subkeys[2], (N_TABLE, requests), 0, 1 << 16) * requests + jnp.arange(requests, dtype=jnp.int32)[None, :]
    positions = jnp.argsort(shuffle_keys, axis=1)
    owner_of = jnp.take_along_axis(owner_of, positions, axis=1)
    local_row = jax.random.randint(subkeys[3], (N_TABLE, requests), 0, ROWS_DEV)
    return (owner_of * ROWS_DEV + local_row).reshape(N_TABLE * SEQ_DEV, LOOKUPS).astype(jnp.int32)


def plant(result, stream_key, low, largest):
    place = [jax.random.randint(jax.random.fold_in(stream_key, axis), (), 0, length) for axis, length in enumerate(result.shape)]
    main_axis = result.shape.index(max(result.shape))
    next_to = place[:main_axis] + [(place[main_axis] + 1) % result.shape[main_axis]] + place[main_axis + 1:]
    return result.at[tuple(place)].set(low).at[tuple(next_to)].set(largest)


def steps_of(stream_key, extent, shards, low, top_value):
    factor_of = 1.0
    for position, shards_of in shards:
        steps = jax.random.uniform(jax.random.fold_in(jax.random.fold_in(stream_key, 6), position), (shards_of,), jnp.float32, low / len(shards), top_value / len(shards))
        factor_of = factor_of * jnp.repeat(jnp.exp(steps), extent[position] // shards_of).reshape((-1,) + (1,) * (len(extent) - 1 - position))
    return factor_of


def centred(rng, shape, deviation, most, shards=(), kind=jnp.bfloat16):
    drawn = jax.random.normal(rng, shape, jnp.float32) * deviation
    if len(shards) > 0:
        drawn = steps_of(rng, shape, shards, -0.22, 0.18) * drawn
    return jnp.clip(drawn, min=-most, max=most).astype(kind)


def setup_inputs(seed: int = 0) -> dict:
    key_of = jax.random.split(jax.random.key(seed), 13)
    hidden = draw_hidden(jax.random.fold_in(key_of[12], 71), 0)
    attn_gain = draw_attn_gain(jax.random.fold_in(key_of[12], 71), 0)
    q_weight = draw_q_weight(jax.random.fold_in(key_of[12], 71), 0)
    kv_weight = centred(key_of[3], (D, 2, KV_HEADS * HEAD_DIM), D ** -0.5, 0.125, ((2, 2),))
    out_weight = centred(key_of[4], (HEADS * HEAD_DIM, D), (HEADS * HEAD_DIM) ** -0.5, 0.125, ((0, 2),))
    key_cache = draw_key_cache(jax.random.fold_in(key_of[12], 71), 0)
    value_cache = centred(key_of[6], (SEQS, CTX, KV_HEADS * HEAD_DIM), 1.0, 6.0, ((0, 16), (2, 2)))
    cache_lengths = plant(jax.random.randint(key_of[7], (SEQS,), CTX // 4, CTX + 1), jax.random.fold_in(key_of[7], 1), CTX // 4, CTX).astype(jnp.int32)
    table = centred(key_of[8], (ROWS, EMB), 1.0, 6.0, ((0, 16),))
    key_proj = centred(key_of[9], (EMB, D), EMB ** -0.5, 0.15625, ((1, 2),))
    value_proj = centred(key_of[10], (EMB, D), EMB ** -0.5, 0.15625, ((1, 2),))
    lookup_ids = draw_lookup_ids(jax.random.fold_in(key_of[12], 71), 0)
    return {"hidden": hidden, "attn_gain": attn_gain, "q_weight": q_weight, "kv_weight": kv_weight, "out_weight": out_weight, "key_cache": key_cache, "value_cache": value_cache, "cache_lengths": cache_lengths, "table": table, "key_proj": key_proj, "value_proj": value_proj, "lookup_ids": lookup_ids}


epsilon = 1e-06

def attend(sequence_item):
    query_heads, new_key, new_value, key_rows, value_rows, length = sequence_item
    group_size = HEADS // KV_HEADS
    inv_scale = 1.0 / math.sqrt(HEAD_DIM)
    query_f = query_heads.astype(jnp.float32).reshape(KV_HEADS, group_size, HEAD_DIM)
    key_f = key_rows.astype(jnp.float32)
    value_f = value_rows.astype(jnp.float32)
    attention_energies = jnp.einsum('kgh,ckh->kgc', query_f, key_f) * inv_scale
    own_score = jnp.einsum('kgh,kh->kg', query_f, new_key.astype(jnp.float32)) * inv_scale
    valid_mask = jnp.arange(CTX, dtype=jnp.int32) < length
    masked = jnp.where(valid_mask[None, None, :], attention_energies, -1e+30)
    row_max = jnp.maximum(lax.optimization_barrier(jnp.max(masked, axis=-1)), own_score)
    weights = jnp.exp(masked - row_max[..., None])
    own_weight = jnp.exp(own_score - row_max)
    denom_sum = lax.optimization_barrier(jnp.sum(weights, axis=-1)) + own_weight
    weights_bf = (weights / denom_sum[..., None]).astype(jnp.bfloat16)
    own_prob = (own_weight / denom_sum).astype(jnp.bfloat16)
    context = jnp.einsum('kgc,ckh->kgh', weights_bf.astype(jnp.float32), value_f)
    context = context + own_prob.astype(jnp.float32)[..., None] * new_value.astype(jnp.float32)[:, None, :]
    return context.reshape(HEADS * HEAD_DIM).astype(jnp.bfloat16)

def reference(hidden, attn_gain, q_weight, kv_weight, out_weight, key_cache, value_cache, cache_lengths, table, key_proj, value_proj, lookup_ids):
    hidden_f32 = hidden.astype(jnp.float32)
    normed = hidden_f32 * lax.rsqrt(lax.optimization_barrier(jnp.mean(hidden_f32 * hidden_f32, axis=1, keepdims=True)) + epsilon)
    attn_in = (normed * attn_gain).astype(jnp.bfloat16)
    query_proj = jnp.dot(attn_in, q_weight, preferred_element_type=jnp.float32).astype(jnp.bfloat16)
    query_proj = query_proj.reshape(SEQS, HEADS, HEAD_DIM)
    kv_cols = KV_HEADS * HEAD_DIM
    new_kv = jnp.dot(attn_in, kv_weight.reshape(D, 2 * kv_cols), preferred_element_type=jnp.float32).astype(jnp.bfloat16)
    new_key = new_kv[:, :kv_cols].reshape(SEQS, KV_HEADS, HEAD_DIM)
    new_value = new_kv[:, kv_cols:].reshape(SEQS, KV_HEADS, HEAD_DIM)
    key_rows = key_cache.reshape(SEQS, CTX, KV_HEADS, HEAD_DIM)
    value_rows = value_cache.reshape(SEQS, CTX, KV_HEADS, HEAD_DIM)
    context = lax.map(attend, (query_proj, new_key, new_value, key_rows, value_rows, cache_lengths))
    attention = jnp.dot(context, out_weight, preferred_element_type=jnp.float32)
    rows = table[lookup_ids.reshape(-1)]
    mem_key = jnp.dot(rows, key_proj, preferred_element_type=jnp.float32).reshape(SEQS, LOOKUPS, D)
    mem_value = jnp.dot(rows, value_proj, preferred_element_type=jnp.float32).reshape(SEQS, LOOKUPS, D)
    cross_term = lax.optimization_barrier(jnp.sum(mem_key * normed[:, None, :], axis=-1))
    square_sum = lax.optimization_barrier(jnp.sum(mem_key * mem_key, axis=-1))
    gating = jax.nn.sigmoid(cross_term * lax.rsqrt(square_sum / D + epsilon) / math.sqrt(D))
    memory = lax.optimization_barrier(jnp.sum(gating[..., None] * mem_value, axis=1))
    return (hidden_f32 + attention + memory).astype(jnp.bfloat16)
```

```python
import math

import jax
import jax.numpy as jnp
from jax import lax
from jax.experimental import pallas as pl
from jax.experimental.pallas import tpu as pltpu
from jax.sharding import PartitionSpec as P

HEAD_DIM = 128


epsilon = 1e-06
VMEM_SPEC = pl.BlockSpec(memory_space=pltpu.VMEM)


def exchange(x, axis, cid, gather=False):
    n = lax.axis_size(axis)

    def kernel(x_ref, o_ref, send, recv, here):
        me = lax.axis_index(axis)
        peers = [lax.rem(me + k, n) for k in range(1, n)]
        barrier = pltpu.get_barrier_semaphore()
        for peer in peers:
            pl.semaphore_signal(barrier, inc=1, device_id={axis: peer})
        pl.semaphore_wait(barrier, n - 1)
        copies = []
        for k, peer in enumerate(peers):
            copy = pltpu.make_async_remote_copy(
                src_ref=x_ref if gather else x_ref.at[peer],
                dst_ref=o_ref.at[me],
                send_sem=send.at[k],
                recv_sem=recv.at[k],
                device_id={axis: peer},
            )
            copy.start()
            copies.append(copy)
        own = pltpu.make_async_copy(x_ref if gather else x_ref.at[me], o_ref.at[me], here)
        own.start()
        own.wait()
        for copy in copies:
            copy.wait()

    shape = (n,) + x.shape if gather else x.shape
    return pl.pallas_call(
        kernel,
        out_shape=jax.ShapeDtypeStruct(shape, x.dtype),
        in_specs=[VMEM_SPEC],
        out_specs=VMEM_SPEC,
        scratch_shapes=[
            pltpu.SemaphoreType.DMA((n - 1,)),
            pltpu.SemaphoreType.DMA((n - 1,)),
            pltpu.SemaphoreType.DMA,
        ],
        compiler_params=pltpu.CompilerParams(collective_id=cid, has_side_effects=True),
    )(x)


def pick_rows(ids, table, column, width):
    count = ids.shape[0]
    rows = table.shape[0]
    chunk = math.gcd(rows, 1024)
    steps = rows // chunk

    def kernel(column_ref, ids_ref, table_ref, o_ref, acc):
        step = pl.program_id(0)
        lanes = lax.broadcasted_iota(jnp.int32, (count, chunk), 1) + step * chunk
        hot = jnp.where(ids_ref[...] == lanes, 1.0, 0.0).astype(jnp.bfloat16)
        part = jnp.dot(hot, table_ref[...], preferred_element_type=jnp.float32)

        @pl.when(step == 0)
        def _():
            acc[...] = part

        @pl.when(step > 0)
        def _():
            acc[...] += part

        @pl.when(step == steps - 1)
        def _():
            o_ref[...] = acc[...].astype(o_ref.dtype)

    return pl.pallas_call(
        kernel,
        grid_spec=pltpu.PrefetchScalarGridSpec(
            num_scalar_prefetch=1,
            grid=(steps,),
            in_specs=[
                pl.BlockSpec((count, 1), lambda i, c: (0, 0)),
                pl.BlockSpec((chunk, width), lambda i, c: (i, c[0])),
            ],
            out_specs=pl.BlockSpec((count, width), lambda i, c: (0, 0)),
            scratch_shapes=[pltpu.VMEM((count, width), jnp.float32)],
        ),
        out_shape=jax.ShapeDtypeStruct((count, width), table.dtype),
    )(column.reshape(1), ids.reshape(count, 1), table)


def local(
    hidden,
    attn_gain,
    q_weight,
    kv_weight,
    out_weight,
    key_cache,
    value_cache,
    cache_lengths,
    table,
    key_proj,
    value_proj,
    lookup_ids,
):
    seq_count, width = hidden.shape
    tensor_count = lax.axis_size("tensor")
    tensor_index = lax.axis_index("tensor")
    slice_width = width // tensor_count
    hidden_f32 = hidden.astype(jnp.float32)
    normed = hidden_f32 * lax.rsqrt(
        jnp.mean(hidden_f32 * hidden_f32, axis=1, keepdims=True) + epsilon
    )
    attn_in = (normed * attn_gain).astype(jnp.bfloat16)
    head_dim = HEAD_DIM
    ctx_len = key_cache.shape[1]
    kv_width = kv_weight.shape[2]
    kv_local = kv_width // head_dim
    group_size = q_weight.shape[1] // kv_width
    inv_scale = 1.0 / math.sqrt(head_dim)
    query_proj = jnp.dot(attn_in, q_weight, preferred_element_type=jnp.float32).astype(jnp.bfloat16)
    new_kv = jnp.dot(
        attn_in, kv_weight.reshape(width, 2 * kv_width), preferred_element_type=jnp.float32
    ).astype(jnp.bfloat16)
    query_heads = query_proj.reshape(seq_count, kv_local, group_size, head_dim)
    new_key = new_kv[:, :kv_width].reshape(seq_count, kv_local, head_dim)
    new_value = new_kv[:, kv_width:].reshape(seq_count, kv_local, head_dim)
    key_blocks = key_cache.reshape(seq_count, ctx_len, kv_local, head_dim)
    value_blocks = value_cache.reshape(seq_count, ctx_len, kv_local, head_dim)
    attention_energies = (
        jnp.einsum("skgh,sckh->skgc", query_heads, key_blocks, preferred_element_type=jnp.float32)
        * inv_scale
    )
    own_score = (
        jnp.einsum("skgh,skh->skg", query_heads, new_key, preferred_element_type=jnp.float32)
        * inv_scale
    )
    valid_mask = jnp.arange(ctx_len, dtype=jnp.int32)[None, :] < cache_lengths[:, None]
    masked = jnp.where(valid_mask[:, None, None, :], attention_energies, -1e30)
    row_max = jnp.maximum(jnp.max(masked, axis=-1), own_score)
    weights = jnp.exp(masked - row_max[..., None])
    own_weight = jnp.exp(own_score - row_max)
    denom_sum = jnp.sum(weights, axis=-1) + own_weight
    weights_bf = (weights / denom_sum[..., None]).astype(jnp.bfloat16)
    own_prob = (own_weight / denom_sum).astype(jnp.bfloat16)
    context = jnp.einsum(
        "skgc,sckh->skgh", weights_bf, value_blocks, preferred_element_type=jnp.float32
    )
    context = (
        context
        + own_prob.astype(jnp.float32)[..., None] * new_value.astype(jnp.float32)[:, :, None, :]
    )
    context = context.reshape(seq_count, -1).astype(jnp.bfloat16)
    attention = jnp.dot(context, out_weight, preferred_element_type=jnp.float32)
    rows_dev, emb_width = table.shape
    table_count = lax.axis_size("table")
    flat_ids = lookup_ids.reshape(-1)
    requests = flat_ids.shape[0]
    capacity = max(2, 2 * requests // table_count)
    owner_of = flat_ids // rows_dev
    local_row = flat_ids - owner_of * rows_dev
    positions = jnp.arange(requests, dtype=jnp.int32)
    earlier = (owner_of[None, :] == owner_of[:, None]) & (positions[None, :] < positions[:, None])
    rank_of = jnp.sum(earlier.astype(jnp.int32), axis=1)
    slot_of = owner_of * capacity + rank_of
    slots = jnp.arange(table_count * capacity, dtype=jnp.int32)
    outgoing = jnp.max(jnp.where(slots[:, None] == slot_of[None, :], local_row[None, :], -1), axis=1)
    outgoing = outgoing.reshape(table_count, 1, capacity)
    outgoing = jnp.pad(outgoing, ((0, 0), (0, 0), (0, -capacity % 128)), constant_values=-1)
    part_width = emb_width // tensor_count
    asked = exchange(outgoing, "table", 0)[:, 0, :capacity].reshape(-1)
    if part_width % 128 == 0:
        wanted = pick_rows(asked, table, tensor_index, part_width)
    else:
        wanted = pick_rows(asked, table, jnp.zeros_like(tensor_index), emb_width)
        wanted = lax.dynamic_slice_in_dim(wanted, tensor_index * part_width, part_width, 1)
    replies = exchange(wanted.reshape(table_count, capacity, part_width), "table", 1)
    chosen = (slot_of[:, None] == slots[None, :]).astype(jnp.bfloat16)
    mem_rows = jnp.dot(
        chosen, replies.reshape(-1, part_width), preferred_element_type=jnp.float32
    ).astype(jnp.bfloat16)
    mem_rows = exchange(mem_rows, "tensor", 2, gather=True)
    mem_rows = jnp.concatenate([mem_rows[j] for j in range(tensor_count)], axis=1)
    lookups = lookup_ids.shape[1]
    mem_key = jnp.dot(mem_rows, key_proj, preferred_element_type=jnp.float32).reshape(
        seq_count, lookups, slice_width
    )
    mem_value = jnp.dot(mem_rows, value_proj, preferred_element_type=jnp.float32).reshape(
        seq_count, lookups, slice_width
    )
    normed_slice = lax.dynamic_slice_in_dim(normed, tensor_index * slice_width, slice_width, 1)
    cross_term = jnp.sum(mem_key * normed_slice[:, None, :], axis=-1)
    square_sum = jnp.sum(mem_key * mem_key, axis=-1)
    both = exchange(jnp.stack([cross_term, square_sum]), "tensor", 3, gather=True)
    cross_term, square_sum = jnp.sum(both, axis=0)
    gating = jax.nn.sigmoid(cross_term * lax.rsqrt(square_sum / width + epsilon) / math.sqrt(width))
    memory = jnp.sum(gating[..., None] * mem_value, axis=1)
    pieces = attention.astype(jnp.bfloat16).reshape(seq_count, tensor_count, slice_width)
    pieces = exchange(jnp.swapaxes(pieces, 0, 1), "tensor", 4)
    attention_part = jnp.sum(pieces.astype(jnp.float32), axis=0)
    residual = lax.dynamic_slice_in_dim(hidden_f32, tensor_index * slice_width, slice_width, 1)
    return (residual + attention_part + memory).astype(jnp.bfloat16)


def solution(mesh):
    return jax.shard_map(
        local,
        mesh=mesh,
        in_specs=(
            P("table", None),
            P(),
            P(None, "tensor"),
            P(None, None, "tensor"),
            P("tensor", None),
            P("table", None, "tensor"),
            P("table", None, "tensor"),
            P("table"),
            P("table", None),
            P(None, "tensor"),
            P(None, "tensor"),
            P("table", None),
        ),
        out_specs=P("table", "tensor"),
        check_vma=False,
    )
```

```python
import math

import jax
import jax.numpy as jnp
from jax import lax
from jax.experimental import pallas as pl
from jax.experimental.pallas import tpu as pltpu
from jax.sharding import PartitionSpec as P

HEAD_DIM = 128


epsilon = 1e-06
VMEM_SPEC = pl.BlockSpec(memory_space=pltpu.VMEM)


def exchange(x, axis, cid, gather=False):
    n = lax.axis_size(axis)

    def kernel(x_ref, o_ref, send, recv, here):
        me = lax.axis_index(axis)
        peers = [lax.rem(me + k, n) for k in range(1, n)]
        barrier = pltpu.get_barrier_semaphore()
        for peer in peers:
            pl.semaphore_signal(barrier, inc=1, device_id={axis: peer})
        pl.semaphore_wait(barrier, n - 1)
        copies = []
        for k, peer in enumerate(peers):
            copy = pltpu.make_async_remote_copy(
                src_ref=x_ref if gather else x_ref.at[peer],
                dst_ref=o_ref.at[me],
                send_sem=send.at[k],
                recv_sem=recv.at[k],
                device_id={axis: peer},
            )
            copy.start()
            copies.append(copy)
        own = pltpu.make_async_copy(x_ref if gather else x_ref.at[me], o_ref.at[me], here)
        own.start()
        own.wait()
        for copy in copies:
            copy.wait()

    shape = (n,) + x.shape if gather else x.shape
    return pl.pallas_call(
        kernel,
        out_shape=jax.ShapeDtypeStruct(shape, x.dtype),
        in_specs=[VMEM_SPEC],
        out_specs=VMEM_SPEC,
        scratch_shapes=[
            pltpu.SemaphoreType.DMA((n - 1,)),
            pltpu.SemaphoreType.DMA((n - 1,)),
            pltpu.SemaphoreType.DMA,
        ],
        compiler_params=pltpu.CompilerParams(collective_id=cid, has_side_effects=True),
    )(x)


def pick_rows(ids, table, column, width):
    count = ids.shape[0]
    rows = table.shape[0]
    chunk = math.gcd(rows, 1024)
    steps = rows // chunk

    def kernel(column_ref, ids_ref, table_ref, o_ref, acc):
        step = pl.program_id(0)
        lanes = lax.broadcasted_iota(jnp.int32, (count, chunk), 1) + step * chunk
        hot = jnp.where(ids_ref[...] == lanes, 1.0, 0.0).astype(jnp.bfloat16)
        part = jnp.dot(hot, table_ref[...], preferred_element_type=jnp.float32)

        @pl.when(step == 0)
        def _():
            acc[...] = part

        @pl.when(step > 0)
        def _():
            acc[...] += part

        @pl.when(step == steps - 1)
        def _():
            o_ref[...] = acc[...].astype(o_ref.dtype)

    return pl.pallas_call(
        kernel,
        grid_spec=pltpu.PrefetchScalarGridSpec(
            num_scalar_prefetch=1,
            grid=(steps,),
            in_specs=[
                pl.BlockSpec((count, 1), lambda i, c: (0, 0)),
                pl.BlockSpec((chunk, width), lambda i, c: (i, c[0])),
            ],
            out_specs=pl.BlockSpec((count, width), lambda i, c: (0, 0)),
            scratch_shapes=[pltpu.VMEM((count, width), jnp.float32)],
        ),
        out_shape=jax.ShapeDtypeStruct((count, width), table.dtype),
    )(column.reshape(1), ids.reshape(count, 1), table)


def greet(axis, peers):
    barrier = pltpu.get_barrier_semaphore()
    for peer in peers:
        pl.semaphore_signal(barrier, inc=1, device_id={axis: peer})
    pl.semaphore_wait(barrier, len(peers))


def attend_and_fetch(hidden, gain, qw, kvw, ow, keys, values, lengths, wanted, slot_of):
    n = lax.axis_size("table")
    pieces = lax.axis_size("tensor")
    seqs, width = hidden.shape
    ctx = keys.shape[1]
    kvw_cols = kvw.shape[1] // 2
    q_cols = qw.shape[1]
    kv_heads = kvw_cols // HEAD_DIM
    heads = q_cols // HEAD_DIM
    group = heads // kv_heads
    pad = -(-heads // 16) * 16
    batch = math.gcd(seqs, 4)
    requests = slot_of.shape[0]
    cap, part = wanted.shape[1:]
    out_cols = width // pieces
    inv_scale = 1.0 / math.sqrt(HEAD_DIM)

    def kernel(
        hid_ref, gain_ref, qw_hbm, kvw_hbm, ow_hbm, k_hbm, v_hbm, len_ref, want_ref, slot_ref,
        rows_ref, att_ref,
        qw_v, kvw_v, ow_v, k_v, v_v, got, qbd, ctxs, nkv, send, recv, sems,
    ):
        me = lax.axis_index("table")
        loads = [
            pltpu.make_async_copy(src, dst, sems.at[i])
            for i, (src, dst) in enumerate(
                [(qw_hbm, qw_v), (kvw_hbm, kvw_v), (k_hbm, k_v), (v_hbm, v_v), (ow_hbm, ow_v)]
            )
        ]
        for load in loads:
            load.start()
        peers = [lax.rem(me + k, n) for k in range(1, n)]
        greet("table", peers)
        copies = []
        for k, peer in enumerate(peers):
            copy = pltpu.make_async_remote_copy(
                src_ref=want_ref.at[peer],
                dst_ref=got.at[me],
                send_sem=send.at[k],
                recv_sem=recv.at[k],
                device_id={"table": peer},
            )
            copy.start()
            copies.append(copy)
        own = pltpu.make_async_copy(want_ref.at[me], got.at[me], sems.at[5])
        own.start()
        hid = hid_ref[...].astype(jnp.float32)
        normed = hid * lax.rsqrt(jnp.mean(hid * hid, axis=1, keepdims=True) + epsilon)
        attn_in = (normed * gain_ref[...]).astype(jnp.bfloat16)
        qbd[...] = jnp.zeros_like(qbd)
        loads[0].wait()
        query = jnp.dot(attn_in, qw_v[...], preferred_element_type=jnp.float32)
        query = query.astype(jnp.bfloat16).astype(jnp.float32)
        for j in range(heads):
            k = j // group
            qbd[k, pl.ds(j, seqs, stride=pad), :] = query[:, j * HEAD_DIM : (j + 1) * HEAD_DIM]
        loads[1].wait()
        new = jnp.dot(attn_in, kvw_v[...], preferred_element_type=jnp.float32)
        new = new.astype(jnp.bfloat16).astype(jnp.float32)
        nkv[0] = new[:, :kvw_cols]
        nkv[1] = new[:, kvw_cols:]
        loads[2].wait()
        loads[3].wait()
        cols = lax.broadcasted_iota(jnp.int32, (1, ctx), 1)

        def step(b, carry):
            masked, own_scores = [], []
            for i in range(batch):
                s = b * batch + i
                at = pl.ds(pl.multiple_of(s * pad, pad), pad)
                q = jnp.concatenate([qbd[k, at, :] for k in range(kv_heads)], axis=1)
                sc = lax.dot_general(
                    q.astype(jnp.bfloat16),
                    k_v[s],
                    (((1,), (1,)), ((), ())),
                    preferred_element_type=jnp.float32,
                )
                masked.append(jnp.where(cols < len_ref[pl.ds(s, 1), :], sc * inv_scale, -1e30))
                new_key = nkv[0, pl.ds(s, 1), :]
                own_scores.append(jnp.sum(q * new_key, axis=1, keepdims=True) * inv_scale)
            masked = jnp.concatenate(masked, axis=0)
            own_score = jnp.concatenate(own_scores, axis=0)
            row_max = jnp.maximum(jnp.max(masked, axis=1, keepdims=True), own_score)
            weights = jnp.exp(masked - row_max)
            own_weight = jnp.exp(own_score - row_max)
            denom = jnp.sum(weights, axis=1, keepdims=True) + own_weight
            probs = (weights / denom).astype(jnp.bfloat16)
            own_prob = (own_weight / denom).astype(jnp.bfloat16).astype(jnp.float32)
            for i in range(batch):
                s = b * batch + i
                c = jnp.dot(
                    probs[i * pad : (i + 1) * pad], v_v[s], preferred_element_type=jnp.float32
                )
                c = c + own_prob[i * pad : (i + 1) * pad] * nkv[1, pl.ds(s, 1), :]
                at = pl.ds(pl.multiple_of(s * pad, pad), pad)
                for k in range(kv_heads):
                    ctxs[k, at, :] = c[:, k * HEAD_DIM : (k + 1) * HEAD_DIM]
            return carry

        lax.fori_loop(0, seqs // batch, step, 0)
        context = jnp.concatenate(
            [ctxs[j // group, pl.ds(j, seqs, stride=pad), :] for j in range(heads)], axis=1
        ).astype(jnp.bfloat16)
        loads[4].wait()
        att = jnp.dot(context, ow_v[...], preferred_element_type=jnp.float32)
        att = att.astype(jnp.bfloat16)
        for t in range(pieces):
            att_ref[t] = att[:, t * out_cols : (t + 1) * out_cols]
        slots = lax.broadcasted_iota(jnp.int32, (requests, n * cap), 1)
        hot = jnp.where(slot_ref[...] == slots, 1.0, 0.0).astype(jnp.bfloat16)
        own.wait()
        for copy in copies:
            copy.wait()
        picked = jnp.dot(
            hot, got[...].reshape(n * cap, part), preferred_element_type=jnp.float32
        )
        rows_ref[...] = picked.astype(jnp.bfloat16)

    hbm = pl.BlockSpec(memory_space=pl.ANY)
    return pl.pallas_call(
        kernel,
        out_shape=[
            jax.ShapeDtypeStruct((requests, part), jnp.bfloat16),
            jax.ShapeDtypeStruct((pieces, seqs, out_cols), jnp.bfloat16),
        ],
        in_specs=[VMEM_SPEC, VMEM_SPEC, hbm, hbm, hbm, hbm, hbm, VMEM_SPEC, VMEM_SPEC, VMEM_SPEC],
        out_specs=[VMEM_SPEC, VMEM_SPEC],
        scratch_shapes=[
            pltpu.VMEM(qw.shape, qw.dtype),
            pltpu.VMEM(kvw.shape, kvw.dtype),
            pltpu.VMEM(ow.shape, ow.dtype),
            pltpu.VMEM(keys.shape, keys.dtype),
            pltpu.VMEM(values.shape, values.dtype),
            pltpu.VMEM(wanted.shape, wanted.dtype),
            pltpu.VMEM((kv_heads, seqs * pad, HEAD_DIM), jnp.float32),
            pltpu.VMEM((kv_heads, seqs * pad, HEAD_DIM), jnp.float32),
            pltpu.VMEM((2, seqs, kvw_cols), jnp.float32),
            pltpu.SemaphoreType.DMA((n - 1,)),
            pltpu.SemaphoreType.DMA((n - 1,)),
            pltpu.SemaphoreType.DMA((6,)),
        ],
        compiler_params=pltpu.CompilerParams(
            collective_id=1, has_side_effects=True, vmem_limit_bytes=60 * 1024 * 1024
        ),
    )(hidden, gain, qw, kvw, ow, keys, values, lengths, wanted, slot_of)


def memory_and_mix(hidden, rows, pieces, key_proj, value_proj):
    n = lax.axis_size("tensor")
    seqs, width = hidden.shape
    requests, part = rows.shape
    lookups = requests // seqs
    cols = width // n

    def split(x):
        high = x.astype(jnp.bfloat16)
        return high, (x - high.astype(jnp.float32)).astype(jnp.bfloat16)

    def dot(a, b):
        return jnp.dot(a, b, preferred_element_type=jnp.float32)

    def kernel(
        hid_ref, rows_ref, att_ref, key_hbm, val_hbm, o_ref,
        key_v, val_v, rows_in, att_in, stat, stat_in, mem_key, sends, recvs, sems,
    ):
        me = lax.axis_index("tensor")
        load_key = pltpu.make_async_copy(key_hbm, key_v, sems.at[0])
        load_val = pltpu.make_async_copy(val_hbm, val_v, sems.at[1])
        load_key.start()
        load_val.start()
        peers = [lax.rem(me + k, n) for k in range(1, n)]
        greet("tensor", peers)

        def start(src, dst, group, k, peer):
            copy = pltpu.make_async_remote_copy(
                src_ref=src,
                dst_ref=dst.at[k],
                send_sem=sends.at[group, k],
                recv_sem=recvs.at[group, k],
                device_id={"tensor": peer},
            )
            copy.start()
            return copy

        row_copies = [start(rows_ref, rows_in, 0, k, p) for k, p in enumerate(peers)]
        att_copies = [start(att_ref.at[p], att_in, 1, k, p) for k, p in enumerate(peers)]
        origins = [lax.rem(me + n - k, n) for k in range(n)]
        held = [rows_ref] + [rows_in.at[k] for k in range(n - 1)]

        def part_of(k):
            return pl.ds(pl.multiple_of(origins[k] * part, math.gcd(part, 128)), part)

        hid = hid_ref[...].astype(jnp.float32)
        scale = lax.rsqrt(jnp.mean(hid * hid, axis=1, keepdims=True) + epsilon)
        mine = pl.ds(pl.multiple_of(me * cols, 128), cols)
        hid_mine = hid_ref[:, mine].astype(jnp.float32)
        normed = hid_mine * scale
        load_key.wait()
        mem_key[...] = dot(rows_ref[...], key_v[part_of(0), :])
        for k, copy in enumerate(row_copies):
            copy.wait()
            mem_key[...] += dot(rows_in[k], key_v[part_of(k + 1), :])
        mk = mem_key[...]
        cross = jnp.sum(mk.reshape(seqs, lookups, cols) * normed[:, None, :], axis=2, keepdims=True)
        square = jnp.sum(mk * mk, axis=1, keepdims=True)
        lane = lax.broadcasted_iota(jnp.int32, (requests, 128), 1)
        both = jnp.where(lane == 0, cross.reshape(requests, 1), square)
        stat[...] = both.T[:8]
        stat_copies = [start(stat, stat_in, 2, k, p) for k, p in enumerate(peers)]
        load_val.wait()
        for copy in att_copies:
            copy.wait()
        total = hid_mine + sum(
            [att_in[k].astype(jnp.float32) for k in range(n - 1)], att_ref[me].astype(jnp.float32)
        )
        sums = stat[...]
        for k, copy in enumerate(stat_copies):
            copy.wait()
            sums = sums + stat_in[k]
        gate = jax.nn.sigmoid(
            sums[0:1] * lax.rsqrt(sums[1:2] / width + epsilon) / math.sqrt(width)
        )
        which = lax.broadcasted_iota(jnp.int32, (seqs, requests), 0) * lookups
        place = lax.broadcasted_iota(jnp.int32, (seqs, requests), 1)
        mask = (place >= which) & (place < which + lookups)
        high, low = split(jnp.where(mask, gate, 0.0))
        for k in range(n):
            r = held[k][...]
            a, b = split(dot(high, r) + dot(low, r))
            v = val_v[part_of(k), :]
            total = total + (dot(a, v) + dot(b, v))
        o_ref[...] = total.astype(o_ref.dtype)

    hbm = pl.BlockSpec(memory_space=pl.ANY)
    return pl.pallas_call(
        kernel,
        out_shape=jax.ShapeDtypeStruct((seqs, cols), jnp.bfloat16),
        in_specs=[VMEM_SPEC, VMEM_SPEC, VMEM_SPEC, hbm, hbm],
        out_specs=VMEM_SPEC,
        scratch_shapes=[
            pltpu.VMEM(key_proj.shape, key_proj.dtype),
            pltpu.VMEM(value_proj.shape, value_proj.dtype),
            pltpu.VMEM((n - 1,) + rows.shape, rows.dtype),
            pltpu.VMEM((n - 1, seqs, cols), jnp.bfloat16),
            pltpu.VMEM((8, requests), jnp.float32),
            pltpu.VMEM((n - 1, 8, requests), jnp.float32),
            pltpu.VMEM((requests, cols), jnp.float32),
            pltpu.SemaphoreType.DMA((3, n - 1)),
            pltpu.SemaphoreType.DMA((3, n - 1)),
            pltpu.SemaphoreType.DMA((2,)),
        ],
        compiler_params=pltpu.CompilerParams(
            collective_id=2, has_side_effects=True, vmem_limit_bytes=48 * 1024 * 1024
        ),
    )(hidden, rows, pieces, key_proj, value_proj)


def local(
    hidden,
    attn_gain,
    q_weight,
    kv_weight,
    out_weight,
    key_cache,
    value_cache,
    cache_lengths,
    table,
    key_proj,
    value_proj,
    lookup_ids,
):
    seq_count, width = hidden.shape
    tensor_count = lax.axis_size("tensor")
    tensor_index = lax.axis_index("tensor")
    kv_width = kv_weight.shape[2]
    rows_dev, emb_width = table.shape
    table_count = lax.axis_size("table")
    flat_ids = lookup_ids.reshape(-1)
    requests = flat_ids.shape[0]
    capacity = max(2, 2 * requests // table_count)
    owner_of = flat_ids // rows_dev
    local_row = flat_ids - owner_of * rows_dev
    positions = jnp.arange(requests, dtype=jnp.int32)
    earlier = (owner_of[None, :] == owner_of[:, None]) & (positions[None, :] < positions[:, None])
    rank_of = jnp.sum(earlier.astype(jnp.int32), axis=1)
    slot_of = owner_of * capacity + rank_of
    slots = jnp.arange(table_count * capacity, dtype=jnp.int32)
    outgoing = jnp.max(jnp.where(slots[:, None] == slot_of[None, :], local_row[None, :], -1), axis=1)
    outgoing = outgoing.reshape(table_count, 1, capacity)
    outgoing = jnp.pad(outgoing, ((0, 0), (0, 0), (0, -capacity % 128)), constant_values=-1)
    part_width = emb_width // tensor_count
    asked = exchange(outgoing, "table", 0)[:, 0, :capacity].reshape(-1)
    if part_width % 128 == 0:
        wanted = pick_rows(asked, table, tensor_index, part_width)
    else:
        wanted = pick_rows(asked, table, jnp.zeros_like(tensor_index), emb_width)
        wanted = lax.dynamic_slice_in_dim(wanted, tensor_index * part_width, part_width, 1)
    lengths = jnp.broadcast_to(cache_lengths[:, None], (seq_count, key_cache.shape[1]))
    mem_rows, pieces = attend_and_fetch(
        hidden,
        attn_gain.reshape(1, width),
        q_weight,
        kv_weight.reshape(width, 2 * kv_width),
        out_weight,
        key_cache,
        value_cache,
        lengths,
        wanted.reshape(table_count, capacity, part_width),
        slot_of.reshape(requests, 1),
    )
    return memory_and_mix(hidden, mem_rows, pieces, key_proj, value_proj)


def solution(mesh):
    return jax.shard_map(
        local,
        mesh=mesh,
        in_specs=(
            P("table", None),
            P(),
            P(None, "tensor"),
            P(None, None, "tensor"),
            P("tensor", None),
            P("table", None, "tensor"),
            P("table", None, "tensor"),
            P("table"),
            P("table", None),
            P(None, "tensor"),
            P(None, "tensor"),
            P("table", None),
        ),
        out_specs=P("table", "tensor"),
        check_vma=False,
    )
```

```python
import math

import jax
import jax.numpy as jnp
from jax import lax
from jax.experimental import pallas as pl
from jax.experimental.pallas import tpu as pltpu
from jax.sharding import PartitionSpec as P

HEAD_DIM = 128


epsilon = 1e-06
VMEM_SPEC = pl.BlockSpec(memory_space=pltpu.VMEM)


def greet(axis, peers):
    barrier = pltpu.get_barrier_semaphore()
    for peer in peers:
        pl.semaphore_signal(barrier, inc=1, device_id={axis: peer})
    pl.semaphore_wait(barrier, len(peers))


def attend_and_fetch(hidden, gain, qw, kvw, ow, keys, values, lengths, table, asks, slot_of, cap):
    n = lax.axis_size("table")
    pieces = lax.axis_size("tensor")
    seqs, width = hidden.shape
    ctx = keys.shape[1]
    kvw_cols = kvw.shape[1] // 2
    q_cols = qw.shape[1]
    kv_heads = kvw_cols // HEAD_DIM
    heads = q_cols // HEAD_DIM
    group = heads // kv_heads
    pad = -(-heads // 16) * 16
    batch = math.gcd(seqs, 4)
    requests = slot_of.shape[0]
    table_rows, emb = table.shape
    part = emb // pieces
    aligned = part % 128 == 0
    held_cols = part if aligned else emb
    chunk = math.gcd(table_rows, 1024)
    owners_at_once = math.gcd(n, max(1, 256 // cap))
    out_cols = width // pieces
    inv_scale = 1.0 / math.sqrt(HEAD_DIM)

    def kernel(
        hid_ref, gain_ref, qw_hbm, kvw_hbm, ow_hbm, k_hbm, v_hbm, table_hbm, len_ref, ask_ref, slot_ref,
        rows_ref, att_ref,
        qw_v, kvw_v, ow_v, k_v, v_v, table_v, asked, want, got, qbd, ctxs, nkv,
        ask_send, ask_recv, send, recv, sems,
    ):
        me = lax.axis_index("table")
        column = lax.axis_index("tensor")
        table_src = table_hbm
        if aligned:
            table_src = table_hbm.at[:, pl.ds(pl.multiple_of(column * part, 128), part)]
        loads = [
            pltpu.make_async_copy(src, dst, sems.at[i])
            for i, (src, dst) in enumerate(
                [
                    (qw_hbm, qw_v),
                    (kvw_hbm, kvw_v),
                    (table_src, table_v),
                    (k_hbm, k_v),
                    (v_hbm, v_v),
                    (ow_hbm, ow_v),
                ]
            )
        ]
        for load in loads:
            load.start()
        peers = [lax.rem(me + k, n) for k in range(1, n)]
        greet("table", peers)
        ask_copies = []
        for k, peer in enumerate(peers):
            copy = pltpu.make_async_remote_copy(
                src_ref=ask_ref.at[k + 1],
                dst_ref=asked.at[k],
                send_sem=ask_send.at[k],
                recv_sem=ask_recv.at[k],
                device_id={"table": peer},
            )
            copy.start()
            ask_copies.append(copy)
        hid = hid_ref[...].astype(jnp.float32)
        normed = hid * lax.rsqrt(jnp.mean(hid * hid, axis=1, keepdims=True) + epsilon)
        attn_in = (normed * gain_ref[...]).astype(jnp.bfloat16)
        qbd[...] = jnp.zeros_like(qbd)
        loads[0].wait()
        query = jnp.dot(attn_in, qw_v[...], preferred_element_type=jnp.float32)
        query = query.astype(jnp.bfloat16).astype(jnp.float32)
        for j in range(heads):
            k = j // group
            qbd[k, pl.ds(j, seqs, stride=pad), :] = query[:, j * HEAD_DIM : (j + 1) * HEAD_DIM]
        loads[1].wait()
        new = jnp.dot(attn_in, kvw_v[...], preferred_element_type=jnp.float32)
        new = new.astype(jnp.bfloat16).astype(jnp.float32)
        nkv[0] = new[:, :kvw_cols]
        nkv[1] = new[:, kvw_cols:]
        for copy in ask_copies:
            copy.wait()
        lanes = ask_ref.shape[2]
        ids = [ask_ref[0]] + [asked[k] for k in range(n - 1)]
        filler = -n % 128
        if filler:
            ids.append(jnp.full((filler, lanes), -1, jnp.int32))
        ids = jnp.concatenate(ids, axis=0).astype(jnp.float32).T.astype(jnp.int32)
        loads[2].wait()
        copies = []
        order = list(range(1, n)) + [0]
        for first in range(0, n, owners_at_once):
            group_ks = order[first : first + owners_at_once]
            wanted = jnp.concatenate([ids[:cap, k : k + 1] for k in group_ks], axis=0)
            picked = None
            for at in range(0, table_rows, chunk):
                row = lax.broadcasted_iota(jnp.int32, (len(group_ks) * cap, chunk), 1) + at
                hot = jnp.where(wanted == row, 1.0, 0.0).astype(jnp.bfloat16)
                term = jnp.dot(
                    hot, table_v[at : at + chunk, :], preferred_element_type=jnp.float32
                )
                picked = term if picked is None else picked + term
            if not aligned:
                mine = picked[:, :part]
                for j in range(1, pieces):
                    mine = jnp.where(column == j, picked[:, j * part : (j + 1) * part], mine)
                picked = mine
            picked = picked.astype(jnp.bfloat16)
            for i, k in enumerate(group_ks):
                block = picked[i * cap : (i + 1) * cap]
                if k == 0:
                    got[0] = block
                    continue
                want[k - 1] = block
            for k in group_ks:
                if k > 0:
                    copy = pltpu.make_async_remote_copy(
                        src_ref=want.at[k - 1],
                        dst_ref=got.at[k],
                        send_sem=send.at[k - 1],
                        recv_sem=recv.at[k - 1],
                        device_id={"table": lax.rem(me + n - k, n)},
                    )
                    copy.start()
                    copies.append(copy)
        loads[3].wait()
        loads[4].wait()
        cols = lax.broadcasted_iota(jnp.int32, (1, ctx), 1)

        def step(b, carry):
            masked, own_scores = [], []
            for i in range(batch):
                s = b * batch + i
                at = pl.ds(pl.multiple_of(s * pad, pad), pad)
                q = jnp.concatenate([qbd[k, at, :] for k in range(kv_heads)], axis=1)
                sc = lax.dot_general(
                    q.astype(jnp.bfloat16),
                    k_v[s],
                    (((1,), (1,)), ((), ())),
                    preferred_element_type=jnp.float32,
                )
                masked.append(jnp.where(cols < len_ref[s], sc * inv_scale, -1e30))
                new_key = nkv[0, pl.ds(s, 1), :]
                own_scores.append(jnp.sum(q * new_key, axis=1, keepdims=True) * inv_scale)
            masked = jnp.concatenate(masked, axis=0)
            own_score = jnp.concatenate(own_scores, axis=0)
            row_max = jnp.maximum(jnp.max(masked, axis=1, keepdims=True), own_score)
            weights = jnp.exp(masked - row_max)
            own_weight = jnp.exp(own_score - row_max)
            denom = jnp.sum(weights, axis=1, keepdims=True) + own_weight
            probs = (weights / denom).astype(jnp.bfloat16)
            own_prob = (own_weight / denom).astype(jnp.bfloat16).astype(jnp.float32)
            for i in range(batch):
                s = b * batch + i
                c = jnp.dot(
                    probs[i * pad : (i + 1) * pad], v_v[s], preferred_element_type=jnp.float32
                )
                c = c + own_prob[i * pad : (i + 1) * pad] * nkv[1, pl.ds(s, 1), :]
                at = pl.ds(pl.multiple_of(s * pad, pad), pad)
                for k in range(kv_heads):
                    ctxs[k, at, :] = c[:, k * HEAD_DIM : (k + 1) * HEAD_DIM]
            return carry

        lax.fori_loop(0, seqs // batch, step, 0)
        context = jnp.concatenate(
            [ctxs[j // group, pl.ds(j, seqs, stride=pad), :] for j in range(heads)], axis=1
        ).astype(jnp.bfloat16)
        loads[5].wait()
        att = jnp.dot(context, ow_v[...], preferred_element_type=jnp.float32)
        att = att.astype(jnp.bfloat16)
        for t in range(pieces):
            att_ref[t] = att[:, t * out_cols : (t + 1) * out_cols]
        slots = lax.broadcasted_iota(jnp.int32, (requests, n * cap), 1)
        hot = jnp.where(slot_ref[...] == slots, 1.0, 0.0).astype(jnp.bfloat16)
        for copy in copies:
            copy.wait()
        picked = jnp.dot(
            hot, got[...].reshape(n * cap, part), preferred_element_type=jnp.float32
        )
        rows_ref[...] = picked.astype(jnp.bfloat16)

    hbm = pl.BlockSpec(memory_space=pl.ANY)
    return pl.pallas_call(
        kernel,
        out_shape=[
            jax.ShapeDtypeStruct((requests, part), jnp.bfloat16),
            jax.ShapeDtypeStruct((pieces, seqs, out_cols), jnp.bfloat16),
        ],
        in_specs=[VMEM_SPEC, VMEM_SPEC]
        + [hbm] * 6
        + [pl.BlockSpec(memory_space=pltpu.SMEM), VMEM_SPEC, VMEM_SPEC],
        out_specs=[VMEM_SPEC, VMEM_SPEC],
        scratch_shapes=[
            pltpu.VMEM(qw.shape, qw.dtype),
            pltpu.VMEM(kvw.shape, kvw.dtype),
            pltpu.VMEM(ow.shape, ow.dtype),
            pltpu.VMEM(keys.shape, keys.dtype),
            pltpu.VMEM(values.shape, values.dtype),
            pltpu.VMEM((table_rows, held_cols), table.dtype),
            pltpu.VMEM((n - 1,) + asks.shape[1:], asks.dtype),
            pltpu.VMEM((n - 1, cap, part), table.dtype),
            pltpu.VMEM((n, cap, part), table.dtype),
            pltpu.VMEM((kv_heads, seqs * pad, HEAD_DIM), jnp.float32),
            pltpu.VMEM((kv_heads, seqs * pad, HEAD_DIM), jnp.float32),
            pltpu.VMEM((2, seqs, kvw_cols), jnp.float32),
            pltpu.SemaphoreType.DMA((n - 1,)),
            pltpu.SemaphoreType.DMA((n - 1,)),
            pltpu.SemaphoreType.DMA((n - 1,)),
            pltpu.SemaphoreType.DMA((n - 1,)),
            pltpu.SemaphoreType.DMA((6,)),
        ],
        compiler_params=pltpu.CompilerParams(
            collective_id=1, has_side_effects=True, vmem_limit_bytes=62 * 1024 * 1024
        ),
    )(hidden, gain, qw, kvw, ow, keys, values, table, lengths, asks, slot_of)


def memory_and_mix(hidden, rows, pieces, key_proj, value_proj):
    n = lax.axis_size("tensor")
    seqs, width = hidden.shape
    requests, part = rows.shape
    lookups = requests // seqs
    cols = width // n

    def split(x):
        high = x.astype(jnp.bfloat16)
        return high, (x - high.astype(jnp.float32)).astype(jnp.bfloat16)

    def dot(a, b):
        return jnp.dot(a, b, preferred_element_type=jnp.float32)

    def kernel(
        hid_ref, rows_ref, att_ref, key_hbm, val_hbm, o_ref,
        key_v, val_v, rows_in, att_in, stat, stat_in, mem_key, sends, recvs, sems,
    ):
        me = lax.axis_index("tensor")
        load_key = pltpu.make_async_copy(key_hbm, key_v, sems.at[0])
        load_val = pltpu.make_async_copy(val_hbm, val_v, sems.at[1])
        load_key.start()
        load_val.start()
        peers = [lax.rem(me + k, n) for k in range(1, n)]
        greet("tensor", peers)

        def start(src, dst, group, k, peer):
            copy = pltpu.make_async_remote_copy(
                src_ref=src,
                dst_ref=dst.at[k],
                send_sem=sends.at[group, k],
                recv_sem=recvs.at[group, k],
                device_id={"tensor": peer},
            )
            copy.start()
            return copy

        row_copies = [start(rows_ref, rows_in, 0, k, p) for k, p in enumerate(peers)]
        att_copies = [start(att_ref.at[p], att_in, 1, k, p) for k, p in enumerate(peers)]
        origins = [lax.rem(me + n - k, n) for k in range(n)]
        held = [rows_ref] + [rows_in.at[k] for k in range(n - 1)]

        def part_of(k):
            return pl.ds(pl.multiple_of(origins[k] * part, math.gcd(part, 128)), part)

        hid = hid_ref[...].astype(jnp.float32)
        scale = lax.rsqrt(jnp.mean(hid * hid, axis=1, keepdims=True) + epsilon)
        mine = pl.ds(pl.multiple_of(me * cols, 128), cols)
        hid_mine = hid_ref[:, mine].astype(jnp.float32)
        normed = hid_mine * scale
        load_key.wait()
        mem_key[...] = dot(rows_ref[...], key_v[part_of(0), :])
        for k, copy in enumerate(row_copies):
            copy.wait()
            mem_key[...] += dot(rows_in[k], key_v[part_of(k + 1), :])
        mk = mem_key[...]
        cross = jnp.sum(mk.reshape(seqs, lookups, cols) * normed[:, None, :], axis=2, keepdims=True)
        square = jnp.sum(mk * mk, axis=1, keepdims=True)
        lane = lax.broadcasted_iota(jnp.int32, (requests, 128), 1)
        both = jnp.where(lane == 0, cross.reshape(requests, 1), square)
        stat[...] = both.T[:8]
        stat_copies = [start(stat, stat_in, 2, k, p) for k, p in enumerate(peers)]
        load_val.wait()
        for copy in att_copies:
            copy.wait()
        total = hid_mine + sum(
            [att_in[k].astype(jnp.float32) for k in range(n - 1)], att_ref[me].astype(jnp.float32)
        )
        sums = stat[...]
        for k, copy in enumerate(stat_copies):
            copy.wait()
            sums = sums + stat_in[k]
        gate = jax.nn.sigmoid(
            sums[0:1] * lax.rsqrt(sums[1:2] / width + epsilon) / math.sqrt(width)
        )
        which = lax.broadcasted_iota(jnp.int32, (seqs, requests), 0) * lookups
        place = lax.broadcasted_iota(jnp.int32, (seqs, requests), 1)
        mask = (place >= which) & (place < which + lookups)
        high, low = split(jnp.where(mask, gate, 0.0))
        for k in range(n):
            r = held[k][...]
            a, b = split(dot(high, r) + dot(low, r))
            v = val_v[part_of(k), :]
            total = total + (dot(a, v) + dot(b, v))
        o_ref[...] = total.astype(o_ref.dtype)

    hbm = pl.BlockSpec(memory_space=pl.ANY)
    return pl.pallas_call(
        kernel,
        out_shape=jax.ShapeDtypeStruct((seqs, cols), jnp.bfloat16),
        in_specs=[VMEM_SPEC, VMEM_SPEC, VMEM_SPEC, hbm, hbm],
        out_specs=VMEM_SPEC,
        scratch_shapes=[
            pltpu.VMEM(key_proj.shape, key_proj.dtype),
            pltpu.VMEM(value_proj.shape, value_proj.dtype),
            pltpu.VMEM((n - 1,) + rows.shape, rows.dtype),
            pltpu.VMEM((n - 1, seqs, cols), jnp.bfloat16),
            pltpu.VMEM((8, requests), jnp.float32),
            pltpu.VMEM((n - 1, 8, requests), jnp.float32),
            pltpu.VMEM((requests, cols), jnp.float32),
            pltpu.SemaphoreType.DMA((3, n - 1)),
            pltpu.SemaphoreType.DMA((3, n - 1)),
            pltpu.SemaphoreType.DMA((2,)),
        ],
        compiler_params=pltpu.CompilerParams(
            collective_id=2, has_side_effects=True, vmem_limit_bytes=62 * 1024 * 1024
        ),
    )(hidden, rows, pieces, key_proj, value_proj)


def local(
    hidden,
    attn_gain,
    q_weight,
    kv_weight,
    out_weight,
    key_cache,
    value_cache,
    cache_lengths,
    table,
    key_proj,
    value_proj,
    lookup_ids,
):
    seq_count, width = hidden.shape
    kv_width = kv_weight.shape[2]
    rows_dev = table.shape[0]
    table_count = lax.axis_size("table")
    flat_ids = lookup_ids.reshape(-1)
    requests = flat_ids.shape[0]
    capacity = max(2, 2 * requests // table_count)
    owner_of = flat_ids // rows_dev
    local_row = flat_ids - owner_of * rows_dev
    positions = jnp.arange(requests, dtype=jnp.int32)
    earlier = (owner_of[None, :] == owner_of[:, None]) & (positions[None, :] < positions[:, None])
    rank_of = jnp.sum(earlier.astype(jnp.int32), axis=1)
    turn = lax.rem(owner_of - lax.axis_index("table") + table_count, table_count)
    slot_of = turn * capacity + rank_of
    slots = jnp.arange(table_count * capacity, dtype=jnp.int32)
    outgoing = jnp.max(jnp.where(slots[:, None] == slot_of[None, :], local_row[None, :], -1), axis=1)
    outgoing = outgoing.reshape(table_count, 1, capacity)
    outgoing = jnp.pad(outgoing, ((0, 0), (0, 0), (0, -capacity % 128)), constant_values=-1)
    mem_rows, pieces = attend_and_fetch(
        hidden,
        attn_gain.reshape(1, width),
        q_weight,
        kv_weight.reshape(width, 2 * kv_width),
        out_weight,
        key_cache,
        value_cache,
        cache_lengths,
        table,
        outgoing,
        slot_of.reshape(requests, 1),
        capacity,
    )
    return memory_and_mix(hidden, mem_rows, pieces, key_proj, value_proj)


def solution(mesh):
    return jax.shard_map(
        local,
        mesh=mesh,
        in_specs=(
            P("table", None),
            P(),
            P(None, "tensor"),
            P(None, None, "tensor"),
            P("tensor", None),
            P("table", None, "tensor"),
            P("table", None, "tensor"),
            P("table"),
            P("table", None),
            P(None, "tensor"),
            P(None, "tensor"),
            P("table", None),
        ),
        out_specs=P("table", "tensor"),
        check_vma=False,
    )
```

```python
import math

import jax
import jax.numpy as jnp
from jax import lax
from jax.experimental import pallas as pl
from jax.experimental.pallas import tpu as pltpu
from jax.sharding import PartitionSpec as P

HEAD_DIM = 128


epsilon = 1e-06
VMEM_SPEC = pl.BlockSpec(memory_space=pltpu.VMEM)


def greet(axis, peers):
    barrier = pltpu.get_barrier_semaphore()
    for peer in peers:
        pl.semaphore_signal(barrier, inc=1, device_id={axis: peer})
    pl.semaphore_wait(barrier, len(peers))


def attend_and_fetch(hidden, gain, qw, kvw, ow, keys, values, lengths, table, asks, slot_of, cap):
    n = lax.axis_size("table")
    pieces = lax.axis_size("tensor")
    seqs, width = hidden.shape
    ctx = keys.shape[1]
    kvw_cols = kvw.shape[1] // 2
    q_cols = qw.shape[1]
    kv_heads = kvw_cols // HEAD_DIM
    heads = q_cols // HEAD_DIM
    group = heads // kv_heads
    pad = -(-heads // 16) * 16
    batch = math.gcd(seqs, 4)
    requests = slot_of.shape[0]
    table_rows, emb = table.shape
    part = emb // pieces
    aligned = part % 128 == 0
    held_cols = part if aligned else emb
    chunk = math.gcd(table_rows, 1024)
    owners_at_once = math.gcd(n, max(1, 256 // cap))
    out_cols = width // pieces
    inv_scale = 1.0 / math.sqrt(HEAD_DIM)

    def kernel(
        hid_ref, gain_ref, qw_hbm, kvw_hbm, ow_hbm, k_hbm, v_hbm, table_hbm, len_ref, ask_ref, slot_ref,
        rows_ref, att_ref,
        qw_v, kvw_v, ow_v, k_v, v_v, table_v, asked, want, got, qbd, ctxs, nkv,
        ask_send, ask_recv, send, recv, sems,
    ):
        me = lax.axis_index("table")
        column = lax.axis_index("tensor")
        table_src = table_hbm
        if aligned:
            table_src = table_hbm.at[:, pl.ds(pl.multiple_of(column * part, 128), part)]
        loads = [
            pltpu.make_async_copy(src, dst, sems.at[i])
            for i, (src, dst) in enumerate(
                [
                    (qw_hbm, qw_v),
                    (kvw_hbm, kvw_v),
                    (table_src, table_v),
                    (k_hbm, k_v),
                    (v_hbm, v_v),
                    (ow_hbm, ow_v),
                ]
            )
        ]
        loads[2].start()
        peers = [lax.rem(me + k, n) for k in range(1, n)]
        greet("table", peers)
        ask_copies = []
        for k, peer in enumerate(peers):
            copy = pltpu.make_async_remote_copy(
                src_ref=ask_ref.at[k + 1],
                dst_ref=asked.at[k],
                send_sem=ask_send.at[k],
                recv_sem=ask_recv.at[k],
                device_id={"table": peer},
            )
            copy.start()
            ask_copies.append(copy)
        for copy in ask_copies:
            copy.wait()
        lanes = ask_ref.shape[2]
        ids = [ask_ref[0]] + [asked[k] for k in range(n - 1)]
        filler = -n % 128
        if filler:
            ids.append(jnp.full((filler, lanes), -1, jnp.int32))
        ids = jnp.concatenate(ids, axis=0).astype(jnp.float32).T.astype(jnp.int32)
        loads[2].wait()
        for i in (0, 1, 3, 4, 5):
            loads[i].start()
        copies = []
        order = sorted(range(1, n), key=lambda k: abs(2 * k - n)) + [0]
        for first in range(0, n, owners_at_once):
            group_ks = order[first : first + owners_at_once]
            wanted = jnp.concatenate([ids[:cap, k : k + 1] for k in group_ks], axis=0)
            picked = None
            for at in range(0, table_rows, chunk):
                row = lax.broadcasted_iota(jnp.int32, (len(group_ks) * cap, chunk), 1) + at
                hot = jnp.where(wanted == row, 1.0, 0.0).astype(jnp.bfloat16)
                term = jnp.dot(
                    hot, table_v[at : at + chunk, :], preferred_element_type=jnp.float32
                )
                picked = term if picked is None else picked + term
            if not aligned:
                mine = picked[:, :part]
                for j in range(1, pieces):
                    mine = jnp.where(column == j, picked[:, j * part : (j + 1) * part], mine)
                picked = mine
            picked = picked.astype(jnp.bfloat16)
            for i, k in enumerate(group_ks):
                block = picked[i * cap : (i + 1) * cap]
                if k == 0:
                    got[0] = block
                    continue
                want[k - 1] = block
            for k in group_ks:
                if k > 0:
                    copy = pltpu.make_async_remote_copy(
                        src_ref=want.at[k - 1],
                        dst_ref=got.at[k],
                        send_sem=send.at[k - 1],
                        recv_sem=recv.at[k - 1],
                        device_id={"table": lax.rem(me + n - k, n)},
                    )
                    copy.start()
                    copies.append(copy)
        hid = hid_ref[...].astype(jnp.float32)
        normed = hid * lax.rsqrt(jnp.mean(hid * hid, axis=1, keepdims=True) + epsilon)
        attn_in = (normed * gain_ref[...]).astype(jnp.bfloat16)
        qbd[...] = jnp.zeros_like(qbd)
        loads[0].wait()
        query = jnp.dot(attn_in, qw_v[...], preferred_element_type=jnp.float32)
        query = query.astype(jnp.bfloat16).astype(jnp.float32)
        for j in range(heads):
            k = j // group
            qbd[k, pl.ds(j, seqs, stride=pad), :] = query[:, j * HEAD_DIM : (j + 1) * HEAD_DIM]
        loads[1].wait()
        new = jnp.dot(attn_in, kvw_v[...], preferred_element_type=jnp.float32)
        new = new.astype(jnp.bfloat16).astype(jnp.float32)
        nkv[0] = new[:, :kvw_cols]
        nkv[1] = new[:, kvw_cols:]
        loads[3].wait()
        loads[4].wait()
        cols = lax.broadcasted_iota(jnp.int32, (1, ctx), 1)

        def step(b, carry):
            masked, own_scores = [], []
            for i in range(batch):
                s = b * batch + i
                at = pl.ds(pl.multiple_of(s * pad, pad), pad)
                q = jnp.concatenate([qbd[k, at, :] for k in range(kv_heads)], axis=1)
                sc = lax.dot_general(
                    q.astype(jnp.bfloat16),
                    k_v[s],
                    (((1,), (1,)), ((), ())),
                    preferred_element_type=jnp.float32,
                )
                masked.append(jnp.where(cols < len_ref[s], sc * inv_scale, -1e30))
                new_key = nkv[0, pl.ds(s, 1), :]
                own_scores.append(jnp.sum(q * new_key, axis=1, keepdims=True) * inv_scale)
            masked = jnp.concatenate(masked, axis=0)
            own_score = jnp.concatenate(own_scores, axis=0)
            row_max = jnp.maximum(jnp.max(masked, axis=1, keepdims=True), own_score)
            weights = jnp.exp(masked - row_max)
            own_weight = jnp.exp(own_score - row_max)
            denom = jnp.sum(weights, axis=1, keepdims=True) + own_weight
            probs = (weights / denom).astype(jnp.bfloat16)
            own_prob = (own_weight / denom).astype(jnp.bfloat16).astype(jnp.float32)
            for i in range(batch):
                s = b * batch + i
                c = jnp.dot(
                    probs[i * pad : (i + 1) * pad], v_v[s], preferred_element_type=jnp.float32
                )
                c = c + own_prob[i * pad : (i + 1) * pad] * nkv[1, pl.ds(s, 1), :]
                at = pl.ds(pl.multiple_of(s * pad, pad), pad)
                for k in range(kv_heads):
                    ctxs[k, at, :] = c[:, k * HEAD_DIM : (k + 1) * HEAD_DIM]
            return carry

        lax.fori_loop(0, seqs // batch, step, 0)
        context = jnp.concatenate(
            [ctxs[j // group, pl.ds(j, seqs, stride=pad), :] for j in range(heads)], axis=1
        ).astype(jnp.bfloat16)
        loads[5].wait()
        att = jnp.dot(context, ow_v[...], preferred_element_type=jnp.float32)
        att = att.astype(jnp.bfloat16)
        for t in range(pieces):
            att_ref[t] = att[:, t * out_cols : (t + 1) * out_cols]
        slots = lax.broadcasted_iota(jnp.int32, (requests, n * cap), 1)
        hot = jnp.where(slot_ref[...] == slots, 1.0, 0.0).astype(jnp.bfloat16)
        for copy in copies:
            copy.wait()
        picked = jnp.dot(
            hot, got[...].reshape(n * cap, part), preferred_element_type=jnp.float32
        )
        rows_ref[...] = picked.astype(jnp.bfloat16)

    hbm = pl.BlockSpec(memory_space=pl.ANY)
    return pl.pallas_call(
        kernel,
        out_shape=[
            jax.ShapeDtypeStruct((requests, part), jnp.bfloat16),
            jax.ShapeDtypeStruct((pieces, seqs, out_cols), jnp.bfloat16),
        ],
        in_specs=[VMEM_SPEC, VMEM_SPEC]
        + [hbm] * 6
        + [pl.BlockSpec(memory_space=pltpu.SMEM), VMEM_SPEC, VMEM_SPEC],
        out_specs=[VMEM_SPEC, VMEM_SPEC],
        scratch_shapes=[
            pltpu.VMEM(qw.shape, qw.dtype),
            pltpu.VMEM(kvw.shape, kvw.dtype),
            pltpu.VMEM(ow.shape, ow.dtype),
            pltpu.VMEM(keys.shape, keys.dtype),
            pltpu.VMEM(values.shape, values.dtype),
            pltpu.VMEM((table_rows, held_cols), table.dtype),
            pltpu.VMEM((n - 1,) + asks.shape[1:], asks.dtype),
            pltpu.VMEM((n - 1, cap, part), table.dtype),
            pltpu.VMEM((n, cap, part), table.dtype),
            pltpu.VMEM((kv_heads, seqs * pad, HEAD_DIM), jnp.float32),
            pltpu.VMEM((kv_heads, seqs * pad, HEAD_DIM), jnp.float32),
            pltpu.VMEM((2, seqs, kvw_cols), jnp.float32),
            pltpu.SemaphoreType.DMA((n - 1,)),
            pltpu.SemaphoreType.DMA((n - 1,)),
            pltpu.SemaphoreType.DMA((n - 1,)),
            pltpu.SemaphoreType.DMA((n - 1,)),
            pltpu.SemaphoreType.DMA((6,)),
        ],
        compiler_params=pltpu.CompilerParams(
            collective_id=1, has_side_effects=True, vmem_limit_bytes=44 * 1024 * 1024
        ),
    )(hidden, gain, qw, kvw, ow, keys, values, table, lengths, asks, slot_of)


def memory_and_mix(hidden, rows, pieces, key_proj, value_proj):
    n = lax.axis_size("tensor")
    seqs, width = hidden.shape
    requests, part = rows.shape
    lookups = requests // seqs
    cols = width // n

    def split(x):
        high = x.astype(jnp.bfloat16)
        return high, (x - high.astype(jnp.float32)).astype(jnp.bfloat16)

    def dot(a, b):
        return jnp.dot(a, b, preferred_element_type=jnp.float32)

    def kernel(
        hid_ref, rows_ref, att_ref, key_hbm, val_hbm, o_ref,
        key_v, val_v, rows_in, att_in, stat, stat_in, mem_key, sends, recvs, sems,
    ):
        me = lax.axis_index("tensor")
        load_key = pltpu.make_async_copy(key_hbm, key_v, sems.at[0])
        load_val = pltpu.make_async_copy(val_hbm, val_v, sems.at[1])
        load_key.start()
        load_val.start()
        peers = [lax.rem(me + k, n) for k in range(1, n)]
        greet("tensor", peers)

        def start(src, dst, group, k, peer):
            copy = pltpu.make_async_remote_copy(
                src_ref=src,
                dst_ref=dst.at[k],
                send_sem=sends.at[group, k],
                recv_sem=recvs.at[group, k],
                device_id={"tensor": peer},
            )
            copy.start()
            return copy

        row_copies = [start(rows_ref, rows_in, 0, k, p) for k, p in enumerate(peers)]
        att_copies = [start(att_ref.at[p], att_in, 1, k, p) for k, p in enumerate(peers)]
        origins = [lax.rem(me + n - k, n) for k in range(n)]
        held = [rows_ref] + [rows_in.at[k] for k in range(n - 1)]

        def part_of(k):
            return pl.ds(pl.multiple_of(origins[k] * part, math.gcd(part, 128)), part)

        hid = hid_ref[...].astype(jnp.float32)
        scale = lax.rsqrt(jnp.mean(hid * hid, axis=1, keepdims=True) + epsilon)
        mine = pl.ds(pl.multiple_of(me * cols, 128), cols)
        hid_mine = hid_ref[:, mine].astype(jnp.float32)
        normed = hid_mine * scale
        load_key.wait()
        mem_key[...] = dot(rows_ref[...], key_v[part_of(0), :])
        for k, copy in enumerate(row_copies):
            copy.wait()
            mem_key[...] += dot(rows_in[k], key_v[part_of(k + 1), :])
        mk = mem_key[...]
        cross = jnp.sum(mk.reshape(seqs, lookups, cols) * normed[:, None, :], axis=2, keepdims=True)
        square = jnp.sum(mk * mk, axis=1, keepdims=True)
        lane = lax.broadcasted_iota(jnp.int32, (requests, 128), 1)
        both = jnp.where(lane == 0, cross.reshape(requests, 1), square)
        stat[...] = both.T[:8]
        stat_copies = [start(stat, stat_in, 2, k, p) for k, p in enumerate(peers)]
        load_val.wait()
        for copy in att_copies:
            copy.wait()
        total = hid_mine + sum(
            [att_in[k].astype(jnp.float32) for k in range(n - 1)], att_ref[me].astype(jnp.float32)
        )
        sums = stat[...]
        for k, copy in enumerate(stat_copies):
            copy.wait()
            sums = sums + stat_in[k]
        gate = jax.nn.sigmoid(
            sums[0:1] * lax.rsqrt(sums[1:2] / width + epsilon) / math.sqrt(width)
        )
        which = lax.broadcasted_iota(jnp.int32, (seqs, requests), 0) * lookups
        place = lax.broadcasted_iota(jnp.int32, (seqs, requests), 1)
        mask = (place >= which) & (place < which + lookups)
        high, low = split(jnp.where(mask, gate, 0.0))
        for k in range(n):
            r = held[k][...]
            a, b = split(dot(high, r) + dot(low, r))
            v = val_v[part_of(k), :]
            total = total + (dot(a, v) + dot(b, v))
        o_ref[...] = total.astype(o_ref.dtype)

    hbm = pl.BlockSpec(memory_space=pl.ANY)
    return pl.pallas_call(
        kernel,
        out_shape=jax.ShapeDtypeStruct((seqs, cols), jnp.bfloat16),
        in_specs=[VMEM_SPEC, VMEM_SPEC, VMEM_SPEC, hbm, hbm],
        out_specs=VMEM_SPEC,
        scratch_shapes=[
            pltpu.VMEM(key_proj.shape, key_proj.dtype),
            pltpu.VMEM(value_proj.shape, value_proj.dtype),
            pltpu.VMEM((n - 1,) + rows.shape, rows.dtype),
            pltpu.VMEM((n - 1, seqs, cols), jnp.bfloat16),
            pltpu.VMEM((8, requests), jnp.float32),
            pltpu.VMEM((n - 1, 8, requests), jnp.float32),
            pltpu.VMEM((requests, cols), jnp.float32),
            pltpu.SemaphoreType.DMA((3, n - 1)),
            pltpu.SemaphoreType.DMA((3, n - 1)),
            pltpu.SemaphoreType.DMA((2,)),
        ],
        compiler_params=pltpu.CompilerParams(
            collective_id=2, has_side_effects=True, vmem_limit_bytes=40 * 1024 * 1024
        ),
    )(hidden, rows, pieces, key_proj, value_proj)


def local(
    hidden,
    attn_gain,
    q_weight,
    kv_weight,
    out_weight,
    key_cache,
    value_cache,
    cache_lengths,
    table,
    key_proj,
    value_proj,
    lookup_ids,
):
    seq_count, width = hidden.shape
    kv_width = kv_weight.shape[2]
    rows_dev = table.shape[0]
    table_count = lax.axis_size("table")
    flat_ids = lookup_ids.reshape(-1)
    requests = flat_ids.shape[0]
    capacity = max(2, 2 * requests // table_count)
    owner_of = flat_ids // rows_dev
    local_row = flat_ids - owner_of * rows_dev
    positions = jnp.arange(requests, dtype=jnp.int32)
    earlier = (owner_of[None, :] == owner_of[:, None]) & (positions[None, :] < positions[:, None])
    rank_of = jnp.sum(earlier.astype(jnp.int32), axis=1)
    turn = lax.rem(owner_of - lax.axis_index("table") + table_count, table_count)
    slot_of = turn * capacity + rank_of
    slots = jnp.arange(table_count * capacity, dtype=jnp.int32)
    outgoing = jnp.max(jnp.where(slots[:, None] == slot_of[None, :], local_row[None, :], -1), axis=1)
    outgoing = outgoing.reshape(table_count, 1, capacity)
    outgoing = jnp.pad(outgoing, ((0, 0), (0, 0), (0, -capacity % 128)), constant_values=-1)
    mem_rows, pieces = attend_and_fetch(
        hidden,
        attn_gain.reshape(1, width),
        q_weight,
        kv_weight.reshape(width, 2 * kv_width),
        out_weight,
        key_cache,
        value_cache,
        cache_lengths,
        table,
        outgoing,
        slot_of.reshape(requests, 1),
        capacity,
    )
    return memory_and_mix(hidden, mem_rows, pieces, key_proj, value_proj)


def solution(mesh):
    return jax.shard_map(
        local,
        mesh=mesh,
        in_specs=(
            P("table", None),
            P(),
            P(None, "tensor"),
            P(None, None, "tensor"),
            P("tensor", None),
            P("table", None, "tensor"),
            P("table", None, "tensor"),
            P("table"),
            P("table", None),
            P(None, "tensor"),
            P(None, "tensor"),
            P("table", None),
        ),
        out_specs=P("table", "tensor"),
        check_vma=False,
    )
```

```python
import math

import jax
import jax.numpy as jnp
from jax import lax
from jax.experimental import pallas as pl
from jax.experimental.pallas import tpu as pltpu
from jax.sharding import PartitionSpec as P

HEAD_DIM = 128


epsilon = 1e-06
VMEM_SPEC = pl.BlockSpec(memory_space=pltpu.VMEM)


def greet(axis, peers):
    barrier = pltpu.get_barrier_semaphore()
    for peer in peers:
        pl.semaphore_signal(barrier, inc=1, device_id={axis: peer})
    pl.semaphore_wait(barrier, len(peers))


def attend_and_fetch(hidden, gain, qw, kvw, ow, keys, values, lengths, table, asks, slot_of, cap):
    n = lax.axis_size("table")
    pieces = lax.axis_size("tensor")
    seqs, width = hidden.shape
    ctx = keys.shape[1]
    kvw_cols = kvw.shape[1] // 2
    q_cols = qw.shape[1]
    kv_heads = kvw_cols // HEAD_DIM
    heads = q_cols // HEAD_DIM
    group = heads // kv_heads
    pad = -(-heads // 16) * 16
    batch = math.gcd(seqs, 4)
    requests = slot_of.shape[0]
    table_rows, emb = table.shape
    part = emb // pieces
    aligned = part % 128 == 0
    held_cols = part if aligned else emb
    chunk = math.gcd(table_rows, 1024)
    owners_at_once = math.gcd(n, max(1, 256 // cap))
    out_cols = width // pieces
    inv_scale = 1.0 / math.sqrt(HEAD_DIM)

    def kernel(
        hid_ref, gain_ref, qw_hbm, kvw_hbm, ow_hbm, k_hbm, v_hbm, table_hbm, len_ref, ask_ref, slot_ref,
        rows_ref, att_ref,
        qw_v, kvw_v, ow_v, k_v, v_v, table_v, asked, want, got, qbd, ctxs, nkv,
        ask_send, ask_recv, send, recv, sems,
    ):
        me = lax.axis_index("table")
        column = lax.axis_index("tensor")
        table_src = table_hbm
        if aligned:
            table_src = table_hbm.at[:, pl.ds(pl.multiple_of(column * part, 128), part)]
        loads = [
            pltpu.make_async_copy(src, dst, sems.at[i])
            for i, (src, dst) in enumerate(
                [
                    (qw_hbm, qw_v),
                    (kvw_hbm, kvw_v),
                    (table_src, table_v),
                    (k_hbm, k_v),
                    (v_hbm, v_v),
                    (ow_hbm, ow_v),
                ]
            )
        ]
        loads[2].start()
        peers = [lax.rem(me + k, n) for k in range(1, n)]
        greet("table", peers)
        ask_copies = []
        for k, peer in enumerate(peers):
            copy = pltpu.make_async_remote_copy(
                src_ref=ask_ref.at[k + 1],
                dst_ref=asked.at[k],
                send_sem=ask_send.at[k],
                recv_sem=ask_recv.at[k],
                device_id={"table": peer},
            )
            copy.start()
            ask_copies.append(copy)
        for copy in ask_copies:
            copy.wait()
        lanes = ask_ref.shape[2]
        ids = [ask_ref[0]] + [asked[k] for k in range(n - 1)]
        filler = -n % 128
        if filler:
            ids.append(jnp.full((filler, lanes), -1, jnp.int32))
        ids = jnp.concatenate(ids, axis=0).astype(jnp.float32).T.astype(jnp.int32)
        loads[2].wait()
        for i in (0, 1, 3, 4, 5):
            loads[i].start()
        copies = []
        order = sorted(range(1, n), key=lambda k: abs(2 * k - n)) + [0]
        for first in range(0, n, owners_at_once):
            group_ks = order[first : first + owners_at_once]
            wanted = jnp.concatenate([ids[:cap, k : k + 1] for k in group_ks], axis=0)
            picked = None
            for at in range(0, table_rows, chunk):
                row = lax.broadcasted_iota(jnp.int32, (len(group_ks) * cap, chunk), 1) + at
                hot = jnp.where(wanted == row, 1.0, 0.0).astype(jnp.bfloat16)
                term = jnp.dot(
                    hot, table_v[at : at + chunk, :], preferred_element_type=jnp.float32
                )
                picked = term if picked is None else picked + term
            if not aligned:
                mine = picked[:, :part]
                for j in range(1, pieces):
                    mine = jnp.where(column == j, picked[:, j * part : (j + 1) * part], mine)
                picked = mine
            picked = picked.astype(jnp.bfloat16)
            for i, k in enumerate(group_ks):
                block = picked[i * cap : (i + 1) * cap]
                if k == 0:
                    got[0] = block
                    continue
                want[k - 1] = block
            for k in group_ks:
                if k > 0:
                    copy = pltpu.make_async_remote_copy(
                        src_ref=want.at[k - 1],
                        dst_ref=got.at[k],
                        send_sem=send.at[k - 1],
                        recv_sem=recv.at[k - 1],
                        device_id={"table": lax.rem(me + n - k, n)},
                    )
                    copy.start()
                    copies.append(copy)
        hid = hid_ref[...].astype(jnp.float32)
        normed = hid * lax.rsqrt(jnp.mean(hid * hid, axis=1, keepdims=True) + epsilon)
        attn_in = (normed * gain_ref[...]).astype(jnp.bfloat16)
        qbd[...] = jnp.zeros_like(qbd)
        loads[0].wait()
        query = jnp.dot(attn_in, qw_v[...], preferred_element_type=jnp.float32)
        query = query.astype(jnp.bfloat16).astype(jnp.float32)
        for j in range(heads):
            k = j // group
            qbd[k, pl.ds(j, seqs, stride=pad), :] = query[:, j * HEAD_DIM : (j + 1) * HEAD_DIM]
        loads[1].wait()
        new = jnp.dot(attn_in, kvw_v[...], preferred_element_type=jnp.float32)
        new = new.astype(jnp.bfloat16).astype(jnp.float32)
        nkv[0] = new[:, :kvw_cols]
        nkv[1] = new[:, kvw_cols:]
        loads[3].wait()
        loads[4].wait()
        cols = lax.broadcasted_iota(jnp.int32, (1, ctx), 1)

        def step(b, carry):
            masked, own_scores = [], []
            for i in range(batch):
                s = b * batch + i
                at = pl.ds(pl.multiple_of(s * pad, pad), pad)
                q = jnp.concatenate([qbd[k, at, :] for k in range(kv_heads)], axis=1)
                sc = lax.dot_general(
                    q.astype(jnp.bfloat16),
                    k_v[s],
                    (((1,), (1,)), ((), ())),
                    preferred_element_type=jnp.float32,
                )
                masked.append(jnp.where(cols < len_ref[s], sc * inv_scale, -1e30))
                new_key = nkv[0, pl.ds(s, 1), :]
                own_scores.append(jnp.sum(q * new_key, axis=1, keepdims=True) * inv_scale)
            masked = jnp.concatenate(masked, axis=0)
            own_score = jnp.concatenate(own_scores, axis=0)
            row_max = jnp.maximum(jnp.max(masked, axis=1, keepdims=True), own_score)
            weights = jnp.exp(masked - row_max)
            own_weight = jnp.exp(own_score - row_max)
            denom = jnp.sum(weights, axis=1, keepdims=True) + own_weight
            probs = (weights / denom).astype(jnp.bfloat16)
            own_prob = (own_weight / denom).astype(jnp.bfloat16).astype(jnp.float32)
            for i in range(batch):
                s = b * batch + i
                c = jnp.dot(
                    probs[i * pad : (i + 1) * pad], v_v[s], preferred_element_type=jnp.float32
                )
                c = c + own_prob[i * pad : (i + 1) * pad] * nkv[1, pl.ds(s, 1), :]
                at = pl.ds(pl.multiple_of(s * pad, pad), pad)
                for k in range(kv_heads):
                    ctxs[k, at, :] = c[:, k * HEAD_DIM : (k + 1) * HEAD_DIM]
            return carry

        lax.fori_loop(0, seqs // batch, step, 0)
        context = jnp.concatenate(
            [ctxs[j // group, pl.ds(j, seqs, stride=pad), :] for j in range(heads)], axis=1
        ).astype(jnp.bfloat16)
        loads[5].wait()
        att = jnp.dot(context, ow_v[...], preferred_element_type=jnp.float32)
        att = att.astype(jnp.bfloat16)
        for t in range(pieces):
            att_ref[t] = att[:, t * out_cols : (t + 1) * out_cols]
        slots = lax.broadcasted_iota(jnp.int32, (requests, n * cap), 1)
        hot = jnp.where(slot_ref[...] == slots, 1.0, 0.0).astype(jnp.bfloat16)
        early = order[: n - owners_at_once]

        def compact(first, last):
            return jnp.dot(
                hot[:, first * cap : last * cap],
                got[first:last].reshape((last - first) * cap, part),
                preferred_element_type=jnp.float32,
            )

        for copy in copies[: len(early)]:
            copy.wait()
        low, high = min(early), max(early) + 1
        picked = compact(low, high)
        for copy in copies[len(early) :]:
            copy.wait()
        picked = picked + compact(0, low)
        if high < n:
            picked = picked + compact(high, n)
        rows_ref[...] = picked.astype(jnp.bfloat16)

    hbm = pl.BlockSpec(memory_space=pl.ANY)
    return pl.pallas_call(
        kernel,
        out_shape=[
            jax.ShapeDtypeStruct((requests, part), jnp.bfloat16),
            jax.ShapeDtypeStruct((pieces, seqs, out_cols), jnp.bfloat16),
        ],
        in_specs=[VMEM_SPEC, VMEM_SPEC]
        + [hbm] * 6
        + [pl.BlockSpec(memory_space=pltpu.SMEM), VMEM_SPEC, VMEM_SPEC],
        out_specs=[VMEM_SPEC, VMEM_SPEC],
        scratch_shapes=[
            pltpu.VMEM(qw.shape, qw.dtype),
            pltpu.VMEM(kvw.shape, kvw.dtype),
            pltpu.VMEM(ow.shape, ow.dtype),
            pltpu.VMEM(keys.shape, keys.dtype),
            pltpu.VMEM(values.shape, values.dtype),
            pltpu.VMEM((table_rows, held_cols), table.dtype),
            pltpu.VMEM((n - 1,) + asks.shape[1:], asks.dtype),
            pltpu.VMEM((n - 1, cap, part), table.dtype),
            pltpu.VMEM((n, cap, part), table.dtype),
            pltpu.VMEM((kv_heads, seqs * pad, HEAD_DIM), jnp.float32),
            pltpu.VMEM((kv_heads, seqs * pad, HEAD_DIM), jnp.float32),
            pltpu.VMEM((2, seqs, kvw_cols), jnp.float32),
            pltpu.SemaphoreType.DMA((n - 1,)),
            pltpu.SemaphoreType.DMA((n - 1,)),
            pltpu.SemaphoreType.DMA((n - 1,)),
            pltpu.SemaphoreType.DMA((n - 1,)),
            pltpu.SemaphoreType.DMA((6,)),
        ],
        compiler_params=pltpu.CompilerParams(
            collective_id=1, has_side_effects=True, vmem_limit_bytes=44 * 1024 * 1024
        ),
    )(hidden, gain, qw, kvw, ow, keys, values, table, lengths, asks, slot_of)


def memory_and_mix(hidden, rows, pieces, key_proj, value_proj):
    n = lax.axis_size("tensor")
    seqs, width = hidden.shape
    requests, part = rows.shape
    lookups = requests // seqs
    cols = width // n

    def split(x):
        high = x.astype(jnp.bfloat16)
        return high, (x - high.astype(jnp.float32)).astype(jnp.bfloat16)

    def dot(a, b):
        return jnp.dot(a, b, preferred_element_type=jnp.float32)

    def kernel(
        hid_ref, rows_ref, att_ref, key_hbm, val_hbm, o_ref,
        key_v, val_v, rows_in, att_in, stat, stat_in, mem_key, sends, recvs, sems,
    ):
        me = lax.axis_index("tensor")
        load_key = pltpu.make_async_copy(key_hbm, key_v, sems.at[0])
        load_val = pltpu.make_async_copy(val_hbm, val_v, sems.at[1])
        load_key.start()
        load_val.start()
        peers = [lax.rem(me + k, n) for k in range(1, n)]
        greet("tensor", peers)

        def start(src, dst, group, k, peer):
            copy = pltpu.make_async_remote_copy(
                src_ref=src,
                dst_ref=dst.at[k],
                send_sem=sends.at[group, k],
                recv_sem=recvs.at[group, k],
                device_id={"tensor": peer},
            )
            copy.start()
            return copy

        row_copies = [start(rows_ref, rows_in, 0, k, p) for k, p in enumerate(peers)]
        att_copies = [start(att_ref.at[p], att_in, 1, k, p) for k, p in enumerate(peers)]
        origins = [lax.rem(me + n - k, n) for k in range(n)]
        held = [rows_ref] + [rows_in.at[k] for k in range(n - 1)]

        def part_of(k):
            return pl.ds(pl.multiple_of(origins[k] * part, math.gcd(part, 128)), part)

        hid = hid_ref[...].astype(jnp.float32)
        scale = lax.rsqrt(jnp.mean(hid * hid, axis=1, keepdims=True) + epsilon)
        mine = pl.ds(pl.multiple_of(me * cols, 128), cols)
        hid_mine = hid_ref[:, mine].astype(jnp.float32)
        normed = hid_mine * scale
        load_key.wait()
        mem_key[...] = dot(rows_ref[...], key_v[part_of(0), :])
        for k, copy in enumerate(row_copies):
            copy.wait()
            mem_key[...] += dot(rows_in[k], key_v[part_of(k + 1), :])
        mk = mem_key[...]
        cross = jnp.sum(mk.reshape(seqs, lookups, cols) * normed[:, None, :], axis=2, keepdims=True)
        square = jnp.sum(mk * mk, axis=1, keepdims=True)
        lane = lax.broadcasted_iota(jnp.int32, (requests, 128), 1)
        both = jnp.where(lane == 0, cross.reshape(requests, 1), square)
        stat[...] = both.T[:8]
        stat_copies = [start(stat, stat_in, 2, k, p) for k, p in enumerate(peers)]
        load_val.wait()
        for copy in att_copies:
            copy.wait()
        total = hid_mine + sum(
            [att_in[k].astype(jnp.float32) for k in range(n - 1)], att_ref[me].astype(jnp.float32)
        )
        sums = stat[...]
        for k, copy in enumerate(stat_copies):
            copy.wait()
            sums = sums + stat_in[k]
        gate = jax.nn.sigmoid(
            sums[0:1] * lax.rsqrt(sums[1:2] / width + epsilon) / math.sqrt(width)
        )
        which = lax.broadcasted_iota(jnp.int32, (seqs, requests), 0) * lookups
        place = lax.broadcasted_iota(jnp.int32, (seqs, requests), 1)
        mask = (place >= which) & (place < which + lookups)
        high, low = split(jnp.where(mask, gate, 0.0))
        for k in range(n):
            r = held[k][...]
            a, b = split(dot(high, r) + dot(low, r))
            v = val_v[part_of(k), :]
            total = total + (dot(a, v) + dot(b, v))
        o_ref[...] = total.astype(o_ref.dtype)

    hbm = pl.BlockSpec(memory_space=pl.ANY)
    return pl.pallas_call(
        kernel,
        out_shape=jax.ShapeDtypeStruct((seqs, cols), jnp.bfloat16),
        in_specs=[VMEM_SPEC, VMEM_SPEC, VMEM_SPEC, hbm, hbm],
        out_specs=VMEM_SPEC,
        scratch_shapes=[
            pltpu.VMEM(key_proj.shape, key_proj.dtype),
            pltpu.VMEM(value_proj.shape, value_proj.dtype),
            pltpu.VMEM((n - 1,) + rows.shape, rows.dtype),
            pltpu.VMEM((n - 1, seqs, cols), jnp.bfloat16),
            pltpu.VMEM((8, requests), jnp.float32),
            pltpu.VMEM((n - 1, 8, requests), jnp.float32),
            pltpu.VMEM((requests, cols), jnp.float32),
            pltpu.SemaphoreType.DMA((3, n - 1)),
            pltpu.SemaphoreType.DMA((3, n - 1)),
            pltpu.SemaphoreType.DMA((2,)),
        ],
        compiler_params=pltpu.CompilerParams(
            collective_id=2, has_side_effects=True, vmem_limit_bytes=40 * 1024 * 1024
        ),
    )(hidden, rows, pieces, key_proj, value_proj)


def local(
    hidden,
    attn_gain,
    q_weight,
    kv_weight,
    out_weight,
    key_cache,
    value_cache,
    cache_lengths,
    table,
    key_proj,
    value_proj,
    lookup_ids,
):
    seq_count, width = hidden.shape
    kv_width = kv_weight.shape[2]
    rows_dev = table.shape[0]
    table_count = lax.axis_size("table")
    flat_ids = lookup_ids.reshape(-1)
    requests = flat_ids.shape[0]
    capacity = max(2, 2 * requests // table_count)
    owner_of = flat_ids // rows_dev
    local_row = flat_ids - owner_of * rows_dev
    positions = jnp.arange(requests, dtype=jnp.int32)
    earlier = (owner_of[None, :] == owner_of[:, None]) & (positions[None, :] < positions[:, None])
    rank_of = jnp.sum(earlier.astype(jnp.int32), axis=1)
    turn = lax.rem(owner_of - lax.axis_index("table") + table_count, table_count)
    slot_of = turn * capacity + rank_of
    slots = jnp.arange(table_count * capacity, dtype=jnp.int32)
    outgoing = jnp.max(jnp.where(slots[:, None] == slot_of[None, :], local_row[None, :], -1), axis=1)
    outgoing = outgoing.reshape(table_count, 1, capacity)
    outgoing = jnp.pad(outgoing, ((0, 0), (0, 0), (0, -capacity % 128)), constant_values=-1)
    mem_rows, pieces = attend_and_fetch(
        hidden,
        attn_gain.reshape(1, width),
        q_weight,
        kv_weight.reshape(width, 2 * kv_width),
        out_weight,
        key_cache,
        value_cache,
        cache_lengths,
        table,
        outgoing,
        slot_of.reshape(requests, 1),
        capacity,
    )
    return memory_and_mix(hidden, mem_rows, pieces, key_proj, value_proj)


def solution(mesh):
    return jax.shard_map(
        local,
        mesh=mesh,
        in_specs=(
            P("table", None),
            P(),
            P(None, "tensor"),
            P(None, None, "tensor"),
            P("tensor", None),
            P("table", None, "tensor"),
            P("table", None, "tensor"),
            P("table"),
            P("table", None),
            P(None, "tensor"),
            P(None, "tensor"),
            P("table", None),
        ),
        out_specs=P("table", "tensor"),
        check_vma=False,
    )
```
